32 devices in a mesh: row: 4 (over y, x), col: 8 (over z, core).
Axes of the slice: x: 2, y: 2, z: 4, core: 2. Of those that a mesh axis runs over, the one named last changes fastest.
Arguments:
- queries: bfloat16 [32, 128, 512], P('row', 'col'), may hold values from -6 to 6
- keys: bfloat16 [32, 128, 512], P('row', 'col'), may hold values from -6 to 6
- values: bfloat16 [32, 128, 512], P('row', 'col'), may hold values from -6 to 6
- grad_out: bfloat16 [32, 128, 512], P('row', 'col'), may hold values from -6 to 6
- rel_bias: float32 [8, 17, 17], replicated, may hold values from -4 to 4
- occupied: int32 [4, 8], replicated, may hold values 0 or 1
Outputs:
- grad_queries: bfloat16 [32, 128, 512], P('row', 'col')
- grad_keys: bfloat16 [32, 128, 512], P('row', 'col')
- grad_values: bfloat16 [32, 128, 512], P('row', 'col')
- grad_bias: float32 [8, 17, 17], replicated
The draws below stay inside these ranges and needn't reach their ends.
All inputs are finite; a program needn't handle non-finite values.
Results may differ from the reference program's by a relative error of at most 0.015.
Values may be sent and summed in bfloat16 or wider, within the bound.
A program may use at most 64 MiB of HBM per device.

```python
import jax
import jax.numpy as jnp
from jax import lax

HEADS = 8
HEAD_DIM = 64
WIDTH = 512
RAD = 8
WIN = 17
TR = 8
TC = 16
GRID_ROWS = 4
GRID_COLS = 8
NR = 32
NC = 128


def base_draw(key, fold_value):
    values = jax.random.normal(jax.random.fold_in(key, fold_value), (NR, NC, WIDTH), jnp.float32)
    return jnp.clip(values, -6.0, 6.0)


def draw_queries(key, part):
    values = base_draw(key, 3)
    return values.astype(jnp.bfloat16)


def draw_keys(key, part):
    values = base_draw(key, 5)
    return values.astype(jnp.bfloat16)


def plant(array, own_key, low, top_value):
    dims = array.shape
    index_at = [jax.random.randint(jax.random.fold_in(own_key, axis), (), 0, dims[axis]) for axis in range(len(dims))]
    array = array.at[tuple(index_at)].set(low)
    longest = dims.index(max(dims))
    index_at[longest] = (index_at[longest] + 1) % dims[longest]
    return array.at[tuple(index_at)].set(top_value)


def block_scale(stream_key, shape, split, smallest, largest):
    loudness, own = 1.0, jax.random.fold_in(stream_key, 6)
    for axis_at, blocks in split:
        steps = jnp.exp(jax.random.uniform(jax.random.fold_in(own, axis_at), (blocks,), jnp.float32, smallest / len(split), largest / len(split)))
        loudness = loudness * jnp.repeat(steps, shape[axis_at] // blocks).reshape([-1 if axis == axis_at else 1 for axis in range(len(shape))])
    return loudness


def scatter_about(own_key, dims, scale, most, cuts=(), held_as=jnp.bfloat16):
    array = scale * jax.random.normal(own_key, dims, jnp.float32)
    if cuts:
        array = array * block_scale(own_key, dims, cuts, -0.22, 0.18)
    return jnp.clip(array, -most, most).astype(held_as)


def setup_inputs(seed: int = 0) -> dict:
    splits = jax.random.split(jax.random.key(seed), 7)
    return {
        "queries": draw_queries(jax.random.fold_in(splits[6], 71), 0),
        "keys": draw_keys(jax.random.fold_in(splits[6], 71), 0),
        "values": scatter_about(splits[2], (NR, NC, WIDTH), 1.0, 6.0, ((0, 4), (1, 8))),
        "grad_out": scatter_about(splits[3], (NR, NC, WIDTH), 1.0, 6.0, ((0, 4), (1, 8))),
        "rel_bias": scatter_about(splits[4], (HEADS, WIN, WIN), 1.0, 4.0, (), jnp.float32),
        "occupied": plant((jax.random.randint(splits[5], (GRID_ROWS, GRID_COLS), 0, 4) < 3).astype(jnp.int32), jax.random.fold_in(splits[5], 1), 0, 1),
    }


def take_cells(padded, row_shift, col_shift):
    return lax.dynamic_slice(padded, (row_shift, col_shift, jnp.int32(0)), (NR, NC, padded.shape[2]))


def take_plane(padded, row_shift, col_shift):
    return lax.dynamic_slice(padded, (row_shift, col_shift), (NR, NC))


def reference(queries, keys, values, grad_out, rel_bias, occupied):
    score_scale = HEAD_DIM ** -0.5
    filled = jnp.repeat(jnp.repeat(occupied, TR, axis=0), TC, axis=1) > 0
    filled_pad = jnp.pad(filled, RAD)
    offsets = jnp.arange(WIN * WIN, dtype=jnp.int32)
    pad_spec = ((RAD, RAD), (RAD, RAD), (0, 0))

    def split_heads(stacked):
        return jnp.transpose(stacked.astype(jnp.float32).reshape(NR, NC, HEADS, HEAD_DIM), (2, 0, 1, 3))

    def one_head(packed):
        head_query, head_key, head_value, head_grad, head_bias = packed
        key_pad = jnp.pad(head_key, pad_spec)
        value_pad = jnp.pad(head_value, pad_spec)
        flat_bias = head_bias.reshape(WIN * WIN)

        def pair_terms(offset):
            row_shift = (offset // WIN).astype(jnp.int32)
            col_shift = (offset % WIN).astype(jnp.int32)
            usable = take_plane(filled_pad, row_shift, col_shift) & filled
            scores = jnp.sum(head_query * take_cells(key_pad, row_shift, col_shift), axis=-1) * score_scale + flat_bias[offset]
            grad_weights = jnp.sum(head_grad * take_cells(value_pad, row_shift, col_shift), axis=-1)
            return jnp.where(usable, scores, -jnp.inf), grad_weights, usable

        all_scores, all_grads, all_usable = lax.map(pair_terms, offsets)
        row_max = jnp.where(filled, jnp.max(all_scores, axis=0), 0.0)
        exponent = jnp.where(all_usable, jnp.exp(all_scores - row_max), 0.0)
        row_total = jnp.where(filled, jnp.sum(exponent, axis=0), 1.0)
        weights = exponent / row_total
        row_delta = jnp.sum(weights * all_grads, axis=0)
        grad_scores = weights * (all_grads - row_delta)
        grad_bias = jnp.sum(grad_scores, axis=(1, 2)).reshape(WIN, WIN)
        weights_low = lax.optimization_barrier(weights.astype(jnp.bfloat16)).astype(jnp.float32)
        grad_scores_low = lax.optimization_barrier(grad_scores.astype(jnp.bfloat16)).astype(jnp.float32)
        query_pad = jnp.pad(head_query, pad_spec)
        grad_pad = jnp.pad(head_grad, pad_spec)
        scores_pad = jnp.pad(grad_scores_low, ((0, 0), (RAD, RAD), (RAD, RAD)))
        weights_pad = jnp.pad(weights_low, ((0, 0), (RAD, RAD), (RAD, RAD)))

        def gather_grads(carried, offset):
            grad_query, grad_key, grad_value = carried
            row_shift = (offset // WIN).astype(jnp.int32)
            col_shift = (offset % WIN).astype(jnp.int32)
            back_row = (2 * RAD - row_shift).astype(jnp.int32)
            back_col = (2 * RAD - col_shift).astype(jnp.int32)
            grad_query = grad_query + grad_scores_low[offset][..., None] * take_cells(key_pad, row_shift, col_shift)
            grad_key = grad_key + take_plane(scores_pad[offset], back_row, back_col)[..., None] * take_cells(query_pad, back_row, back_col)
            grad_value = grad_value + take_plane(weights_pad[offset], back_row, back_col)[..., None] * take_cells(grad_pad, back_row, back_col)
            return (grad_query, grad_key, grad_value), None

        initial = jnp.zeros((NR, NC, HEAD_DIM), jnp.float32)
        (grad_query, grad_key, grad_value), _ = lax.scan(gather_grads, (initial, initial, initial), offsets)
        return grad_query * score_scale, grad_key * score_scale, grad_value, grad_bias

    all_query, all_key, all_value, all_bias = lax.map(
        one_head, (split_heads(queries), split_heads(keys), split_heads(values), split_heads(grad_out), rel_bias))

    def merge_heads(stacked):
        return jnp.transpose(stacked, (1, 2, 0, 3)).reshape(NR, NC, HEADS * HEAD_DIM).astype(jnp.bfloat16)

    return merge_heads(all_query), merge_heads(all_key), merge_heads(all_value), all_bias
```

```python
import functools

import jax
import jax.numpy as jnp
from jax import lax
from jax.experimental import pallas as pl
from jax.experimental.pallas import tpu as pltpu
from jax.sharding import PartitionSpec as P

MESH = pl.DeviceIdType.MESH
LANES = 128
MASKED = -1e30


def skew_rows(block, direction):
    row = lax.broadcasted_iota(jnp.int32, block.shape, 0)
    span = block.shape[1]
    bit = 1
    while bit < block.shape[0]:
        moved = pltpu.roll(block, (direction * bit) % span, 1)
        block = jnp.where((row & bit) != 0, moved, block)
        bit *= 2
    return block


def kernel(
    cfg,
    q_ref, k_ref, v_ref, g_ref, flat_ref, key_ok_ref, own_ref,
    dq_ref, dk_ref, dv_ref, db_ref,
    row_kv, col_kv, col_out, grad_col_out, grad_col_in, grad_row_out, grad_row_in,
    mid, bias_full, s_buf, gw_buf, w_buf, ds_buf, bias_acc, bias_cols, bias_rows,
    row_kv_s, row_kv_r, col_kv_s, col_kv_r, gc_s, gc_r, gr_s, gr_r, bc_s, bc_r, br_s, br_r,
):
    n_row, n_col, tr, tc, rad, heads, width = cfg
    hd = width // heads
    per = LANES // hd
    groups = width // LANES
    pr, pc = tr + 2 * rad, tc + 2 * rad
    span = pr * pc
    nq = tr * tc
    half = rad * tr
    f32, bf16 = jnp.float32, jnp.bfloat16
    r = lax.axis_index("row")
    c = lax.axis_index("col")
    row_has = (r > 0, r < n_row - 1)
    row_to = (r - 1, r + 1)
    col_has = (c > 0, c < n_col - 1)
    col_to = (c - 1, c + 1)

    row_kv[...] = jnp.zeros_like(row_kv)
    col_kv[...] = jnp.zeros_like(col_kv)
    grad_col_in[...] = jnp.zeros_like(grad_col_in)
    grad_row_in[...] = jnp.zeros_like(grad_row_in)

    barrier = pltpu.get_barrier_semaphore()
    for step in range(1, n_col):
        pl.semaphore_signal(barrier, 1, device_id=(r, lax.rem(c + step, n_col)), device_id_type=MESH)
    for step in range(1, n_row):
        pl.semaphore_signal(barrier, 1, device_id=(lax.rem(r + step, n_row), c), device_id_type=MESH)
    pl.semaphore_wait(barrier, n_col + n_row - 2)

    pending = []

    def send(cond, make):
        @pl.when(cond)
        def _():
            make().start()

        pending.append((cond, make))

    def arrived(cond, make):
        @pl.when(cond)
        def _():
            make().wait_recv()

    def lanes(g):
        return pl.ds(g * LANES, LANES)

    def row_copy(g, d, i):
        src = (k_ref, v_ref)[i]
        return lambda: pltpu.make_async_remote_copy(
            src_ref=src.at[:, lanes(g)], dst_ref=row_kv.at[1 - d, g, i],
            send_sem=row_kv_s.at[d, g, i], recv_sem=row_kv_r.at[1 - d, g, i],
            device_id=(row_to[d], c), device_id_type=MESH)

    def row_wait(g, d, i):
        arrived(row_has[d], lambda: pltpu.make_async_remote_copy(
            src_ref=row_kv.at[d, g, i], dst_ref=row_kv.at[d, g, i],
            send_sem=row_kv_s.at[d, g, i], recv_sem=row_kv_r.at[d, g, i],
            device_id=(row_to[d], c), device_id_type=MESH))

    def tile_of(g, piece, i):
        if piece == 1:
            return (k_ref, v_ref)[i][:, lanes(g)].astype(f32).reshape(tr, tc, LANES)
        return row_kv[0 if piece == 0 else 1, g, i].astype(f32).reshape(tr, tc, LANES)

    def col_copy(g, piece, d):
        return lambda: pltpu.make_async_remote_copy(
            src_ref=col_out.at[d, g, piece], dst_ref=col_kv.at[1 - d, g, piece],
            send_sem=col_kv_s.at[d, g, piece], recv_sem=col_kv_r.at[1 - d, g, piece],
            device_id=(r, col_to[d]), device_id_type=MESH)

    def col_send(g, piece):
        for i in range(2):
            tile = tile_of(g, piece, i)
            col_out[0, g, piece, i] = tile[:, :rad].reshape(half, LANES).astype(bf16)
            col_out[1, g, piece, i] = tile[:, tc - rad:].reshape(half, LANES).astype(bf16)
        for d in range(2):
            send(col_has[d], col_copy(g, piece, d))

    def col_wait(g):
        for piece in range(3):
            for d in range(2):
                arrived(col_has[d], (lambda piece, d: lambda: pltpu.make_async_remote_copy(
                    src_ref=col_kv.at[d, g, piece], dst_ref=col_kv.at[d, g, piece],
                    send_sem=col_kv_s.at[d, g, piece], recv_sem=col_kv_r.at[d, g, piece],
                    device_id=(r, col_to[d]), device_id_type=MESH))(piece, d))

    def row_stage(g):
        for d in range(2):
            for i in range(2):
                row_wait(g, d, i)
        col_send(g, 0)
        col_send(g, 2)

    def window(g, i):
        parts = []
        for piece in range(3):
            left = col_kv[0, g, piece, i].astype(f32).reshape(tr, rad, LANES)
            right = col_kv[1, g, piece, i].astype(f32).reshape(tr, rad, LANES)
            parts.append(jnp.concatenate([left, tile_of(g, piece, i), right], axis=1))
        return jnp.concatenate(parts, axis=0).reshape(span, LANES).astype(bf16)

    def stacked(matrix, scale):
        lane = lax.broadcasted_iota(jnp.int32, (nq, LANES), 1)
        wide = matrix.astype(f32) * scale
        return jnp.concatenate(
            [jnp.where(lane // hd == h, wide, 0.0) for h in range(per)], axis=0).astype(bf16)

    def expand_bias():
        lane = lax.broadcasted_iota(jnp.int32, (tc, span), 1)
        key_col = lax.rem(lane, pc)
        key_row = lane // pc
        query_col = lax.broadcasted_iota(jnp.int32, (tc, span), 0)
        off_col = key_col - query_col
        ok_col = (off_col >= 0) & (off_col <= 2 * rad) & (key_ok_ref[...] > 0.5)

        def one_head(h, _):
            base = jnp.broadcast_to(flat_ref[pl.ds(h, 1), :], (tc, span))
            base = skew_rows(base, 1)
            for qr in range(tr):
                off_row = key_row - qr
                ok = ok_col & (off_row >= 0) & (off_row <= 2 * rad)
                moved = pltpu.roll(base, (pc * qr) % span, 1) if qr else base
                bias_full[h, qr] = jnp.where(ok, moved, MASKED)
            return 0

        lax.fori_loop(0, heads, one_head, 0)

    def compute(g):
        kw = window(g, 0)
        vw = window(g, 1)
        qs = stacked(q_ref[:, lanes(g)], hd ** -0.5)
        gs = stacked(g_ref[:, lanes(g)], 1.0)
        nt = (((1,), (1,)), ((), ()))
        s_buf[...] = lax.dot_general(qs, kw, nt, preferred_element_type=f32)
        gw_buf[...] = lax.dot_general(gs, vw, nt, preferred_element_type=f32)
        bias_acc[...] = jnp.zeros_like(bias_acc)
        own = own_ref[0, 0]

        def chunk(qr, _):
            for h in range(per):
                at = pl.multiple_of(h * nq + qr * tc, tc)
                s = s_buf[pl.ds(at, tc), :] + bias_full[g * per + h, qr]
                e = jnp.exp(s - jnp.max(s, axis=1, keepdims=True))
                w = e * (own / jnp.sum(e, axis=1, keepdims=True))
                gw = gw_buf[pl.ds(at, tc), :]
                ds = w * (gw - jnp.sum(w * gw, axis=1, keepdims=True))
                w_buf[pl.ds(at, tc), :] = w.astype(bf16)
                ds_buf[pl.ds(at, tc), :] = ds.astype(bf16)
                bias_acc[h] += pltpu.roll(ds, lax.rem(span - pc * qr, span), 1)
            return 0

        lax.fori_loop(0, tr, chunk, 0)
        for h in range(per):
            total = jnp.sum(skew_rows(bias_acc[h], -1), axis=0, keepdims=True)
            bias_cols[c, pl.ds(g * per + h, 1), :] = total
        ds_low = ds_buf[...]
        tn = (((0,), (0,)), ((), ()))
        dq = jnp.dot(ds_low, kw, preferred_element_type=f32) * (hd ** -0.5)
        lane = lax.broadcasted_iota(jnp.int32, (nq, LANES), 1)
        merged = dq[:nq]
        for h in range(1, per):
            merged = jnp.where(lane // hd == h, dq[h * nq:(h + 1) * nq], merged)
        dq_ref[:, lanes(g)] = merged.astype(bf16)
        for i, (left, right) in enumerate(((ds_low, qs), (w_buf[...], gs))):
            full = lax.dot_general(left, right, tn, preferred_element_type=f32)
            full = full.reshape(pr, pc, LANES)
            grad_col_out[0, g, i] = full[:, :rad].reshape(pr * rad, LANES).astype(bf16)
            grad_col_out[1, g, i] = full[:, rad + tc:].reshape(pr * rad, LANES).astype(bf16)
            mid[g, i] = full[:, rad:rad + tc]
        for d in range(2):
            send(col_has[d], (lambda d: lambda: pltpu.make_async_remote_copy(
                src_ref=grad_col_out.at[d, g], dst_ref=grad_col_in.at[1 - d, g],
                send_sem=gc_s.at[d, g], recv_sem=gc_r.at[1 - d, g],
                device_id=(r, col_to[d]), device_id_type=MESH))(d))

    def col_return(g):
        for d in range(2):
            arrived(col_has[d], (lambda d: lambda: pltpu.make_async_remote_copy(
                src_ref=grad_col_in.at[d, g], dst_ref=grad_col_in.at[d, g],
                send_sem=gc_s.at[d, g], recv_sem=gc_r.at[d, g],
                device_id=(r, col_to[d]), device_id_type=MESH))(d))
        for i in range(2):
            sides = [grad_col_in[d, g, i].astype(f32).reshape(pr, rad, LANES) for d in range(2)]
            if tc == 2 * rad:
                total = mid[g, i] + jnp.concatenate(sides, axis=1)
            else:
                gap = jnp.zeros((pr, tc - rad, LANES), f32)
                total = (mid[g, i] + jnp.concatenate([sides[0], gap], axis=1)
                         + jnp.concatenate([gap, sides[1]], axis=1))
            grad_row_out[0, g, i] = total[:rad].reshape(nq, LANES).astype(bf16)
            grad_row_out[1, g, i] = total[rad + tr:].reshape(nq, LANES).astype(bf16)
            mid[g, i] = total
        for d in range(2):
            send(row_has[d], (lambda d: lambda: pltpu.make_async_remote_copy(
                src_ref=grad_row_out.at[d, g], dst_ref=grad_row_in.at[1 - d, g],
                send_sem=gr_s.at[d, g], recv_sem=gr_r.at[1 - d, g],
                device_id=(row_to[d], c), device_id_type=MESH))(d))

    def finish(g):
        for d in range(2):
            arrived(row_has[d], (lambda d: lambda: pltpu.make_async_remote_copy(
                src_ref=grad_row_in.at[d, g], dst_ref=grad_row_in.at[d, g],
                send_sem=gr_s.at[d, g], recv_sem=gr_r.at[d, g],
                device_id=(row_to[d], c), device_id_type=MESH))(d))
        for i, out in enumerate((dk_ref, dv_ref)):
            total = mid[g, i, pl.ds(rad, tr)].reshape(nq, LANES)
            total = total + grad_row_in[0, g, i].astype(f32) + grad_row_in[1, g, i].astype(f32)
            out[:, lanes(g)] = total.astype(bf16)

    for g in range(groups):
        for d in range(2):
            for i in range(2):
                send(row_has[d], row_copy(g, d, i))
    for g in range(groups):
        col_send(g, 1)
    expand_bias()
    row_stage(0)
    for g in range(groups):
        if g + 1 < groups:
            row_stage(g + 1)
        col_wait(g)
        compute(g)
        if g >= 1:
            col_return(g - 1)
        if g >= 2:
            finish(g - 2)

    def bias_copies(buf, mine, count, send_sem, recv_sem, device):
        return [pltpu.make_async_remote_copy(
            src_ref=buf.at[mine], dst_ref=buf.at[mine],
            send_sem=send_sem.at[step], recv_sem=recv_sem.at[step],
            device_id=device(lax.rem(mine + step, count)), device_id_type=MESH)
            for step in range(1, count)]

    def bias_waits(buf, mine, count, send_sem, recv_sem, device):
        for step in range(1, count):
            source = lax.rem(mine + count - step, count)
            pltpu.make_async_remote_copy(
                src_ref=buf.at[source], dst_ref=buf.at[source],
                send_sem=send_sem.at[step], recv_sem=recv_sem.at[step],
                device_id=device(source), device_id_type=MESH).wait_recv()

    by_col = (bias_cols, c, n_col, bc_s, bc_r, lambda at: (r, at))
    by_row = (bias_rows, r, n_row, br_s, br_r, lambda at: (at, c))
    col_copies = bias_copies(*by_col)
    for copy in col_copies:
        copy.start()
    col_return(groups - 1)
    if groups >= 2:
        finish(groups - 2)
    bias_waits(*by_col)
    total = bias_cols[0]
    for at in range(1, n_col):
        total = total + bias_cols[at]
    bias_rows[r] = total
    row_copies = bias_copies(*by_row)
    for copy in row_copies:
        copy.start()
    finish(groups - 1)
    bias_waits(*by_row)
    total = bias_rows[0]
    for at in range(1, n_row):
        total = total + bias_rows[at]
    db_ref[...] = total
    for copy in col_copies + row_copies:
        copy.wait_send()
    for cond, make in pending:
        @pl.when(cond)
        def _():
            make().wait_send()


def shards(n_row, n_col, queries, keys, values, grad_out, rel_bias, occupied):
    tr, tc, width = queries.shape
    heads, win, _ = rel_bias.shape
    rad = (win - 1) // 2
    pr, pc = tr + 2 * rad, tc + 2 * rad
    span = pr * pc
    nq = tr * tc
    groups = width // LANES
    per = heads // groups
    half = rad * tr
    r = lax.axis_index("row")
    c = lax.axis_index("col")
    nearby = lax.dynamic_slice(jnp.pad(occupied, 1), (r, c), (3, 3)).astype(jnp.float32)
    row_tile = [0] * rad + [1] * tr + [2] * rad
    col_tile = [0] * rad + [1] * tc + [2] * rad
    rows = jnp.concatenate([jnp.broadcast_to(nearby[i:i + 1], (n, 3)) for i, n in enumerate((rad, tr, rad))], axis=0)
    cells = jnp.concatenate(
        [jnp.broadcast_to(rows[:, i:i + 1], (pr, n)) for i, n in enumerate((rad, tc, rad))], axis=1)
    key_ok = cells.reshape(1, span)
    own = nearby[1:2, 1:2]
    flat = jnp.pad(rel_bias, ((0, 0), (0, pr - win), (0, pc - win))).reshape(heads, span)
    f32, bf16 = jnp.float32, jnp.bfloat16
    vmem = pl.BlockSpec(memory_space=pltpu.VMEM)
    dma = pltpu.SemaphoreType.DMA
    token = jax.ShapeDtypeStruct((nq, width), bf16)
    cfg = (n_row, n_col, tr, tc, rad, heads, width)
    dq, dk, dv, db = pl.pallas_call(
        functools.partial(kernel, cfg),
        out_shape=(token, token, token, jax.ShapeDtypeStruct((heads, span), f32)),
        in_specs=[vmem] * 6 + [pl.BlockSpec(memory_space=pltpu.SMEM)],
        out_specs=(vmem,) * 4,
        scratch_shapes=[
            pltpu.VMEM((2, groups, 2, nq, LANES), bf16),
            pltpu.VMEM((2, groups, 3, 2, half, LANES), bf16),
            pltpu.VMEM((2, groups, 3, 2, half, LANES), bf16),
            pltpu.VMEM((2, groups, 2, pr * rad, LANES), bf16),
            pltpu.VMEM((2, groups, 2, pr * rad, LANES), bf16),
            pltpu.VMEM((2, groups, 2, nq, LANES), bf16),
            pltpu.VMEM((2, groups, 2, nq, LANES), bf16),
            pltpu.VMEM((groups, 2, pr, tc, LANES), f32),
            pltpu.VMEM((heads, tr, tc, span), f32),
            pltpu.VMEM((per * nq, span), f32),
            pltpu.VMEM((per * nq, span), f32),
            pltpu.VMEM((per * nq, span), bf16),
            pltpu.VMEM((per * nq, span), bf16),
            pltpu.VMEM((per, tc, span), f32),
            pltpu.VMEM((n_col, heads, span), f32),
            pltpu.VMEM((n_row, heads, span), f32),
            dma((2, groups, 2)), dma((2, groups, 2)),
            dma((2, groups, 3)), dma((2, groups, 3)),
            dma((2, groups)), dma((2, groups)),
            dma((2, groups)), dma((2, groups)),
            dma((n_col,)), dma((n_col,)),
            dma((n_row,)), dma((n_row,)),
        ],
        compiler_params=pltpu.CompilerParams(
            collective_id=0, has_side_effects=True, vmem_limit_bytes=48 * 1024 * 1024),
    )(
        queries.reshape(nq, width), keys.reshape(nq, width), values.reshape(nq, width),
        grad_out.reshape(nq, width), flat, key_ok, own,
    )
    grad_bias = db.reshape(heads, pr, pc)[:, :win, :win]
    shape = (tr, tc, width)
    return dq.reshape(shape), dk.reshape(shape), dv.reshape(shape), grad_bias


def solution(mesh):
    tokens = P("row", "col", None)
    return jax.shard_map(
        functools.partial(shards, mesh.shape["row"], mesh.shape["col"]),
        mesh=mesh,
        in_specs=(tokens,) * 4 + (P(), P()),
        out_specs=(tokens,) * 3 + (P(),),
        check_vma=False,
    )
```

```python
import functools

import jax
import jax.numpy as jnp
from jax import lax
from jax.experimental import pallas as pl
from jax.experimental.pallas import tpu as pltpu
from jax.sharding import PartitionSpec as P

MESH = pl.DeviceIdType.MESH
LANES = 128
MASKED = -1e30


def skew_rows(block, direction):
    row = lax.broadcasted_iota(jnp.int32, block.shape, 0)
    span = block.shape[1]
    bit = 1
    while bit < block.shape[0]:
        moved = pltpu.roll(block, (direction * bit) % span, 1)
        block = jnp.where((row & bit) != 0, moved, block)
        bit *= 2
    return block


def kernel(
    cfg,
    q_hbm, k_hbm, v_hbm, g_hbm, bias_hbm, occ_hbm,
    dq_hbm, dk_hbm, dv_hbm, db_hbm,
    q_ref, k_ref, v_ref, g_ref, bias_ref, occ_ref, dq_ref, dk_ref, dv_ref, db_ref, in_s, out_s,
    row_kv, col_kv, col_out, grad_col_out, grad_col_in, grad_row_out, grad_row_in,
    mid, flat_ref, bias_full, s_buf, gw_buf, w_buf, ds_buf, bias_acc, bias_cols, bias_rows,
    row_kv_s, row_kv_r, col_kv_s, col_kv_r, gc_s, gc_r, gr_s, gr_r, bc_s, bc_r, br_s, br_r,
):
    n_row, n_col, tr, tc, rad, heads, width = cfg
    win = 2 * rad + 1
    hd = width // heads
    per = LANES // hd
    groups = width // LANES
    pr, pc = tr + 2 * rad, tc + 2 * rad
    span = pr * pc
    nq = tr * tc
    half = rad * tr
    f32, bf16 = jnp.float32, jnp.bfloat16
    r = lax.axis_index("row")
    c = lax.axis_index("col")
    row_has = (r > 0, r < n_row - 1)
    row_to = (r - 1, r + 1)
    col_has = (c > 0, c < n_col - 1)
    col_to = (c - 1, c + 1)

    moves = ((k_hbm, k_ref), (v_hbm, v_ref), (occ_hbm, occ_ref), (bias_hbm, bias_ref), (q_hbm, q_ref), (g_hbm, g_ref))
    loads = [pltpu.make_async_copy(a, b, in_s.at[i]) for i, (a, b) in enumerate(moves)]
    for load in loads:
        load.start()

    barrier = pltpu.get_barrier_semaphore()
    for step in range(1, n_col):
        pl.semaphore_signal(barrier, 1, device_id=(r, lax.rem(c + step, n_col)), device_id_type=MESH)
    for step in range(1, n_row):
        pl.semaphore_signal(barrier, 1, device_id=(lax.rem(r + step, n_row), c), device_id_type=MESH)
    pl.semaphore_wait(barrier, n_col + n_row - 2)

    for load in loads[:2]:
        load.wait()
    pending = []
    stores = []

    def send(cond, make):
        @pl.when(cond)
        def _():
            make().start()

        pending.append((cond, make))

    def arrived(cond, make):
        @pl.when(cond)
        def _():
            make().wait_recv()

    def lanes(g):
        return pl.ds(g * LANES, LANES)

    def clear_missing():
        for d in range(2):
            @pl.when(jnp.logical_not(row_has[d]))
            def _():
                row_kv[d] = jnp.zeros_like(row_kv[d])
                grad_row_in[d] = jnp.zeros_like(grad_row_in[d])

            @pl.when(jnp.logical_not(col_has[d]))
            def _():
                col_kv[d] = jnp.zeros_like(col_kv[d])
                grad_col_in[d] = jnp.zeros_like(grad_col_in[d])

    def row_copy(g, d, i):
        src = (k_ref, v_ref)[i]
        return lambda: pltpu.make_async_remote_copy(
            src_ref=src.at[:, lanes(g)], dst_ref=row_kv.at[1 - d, g, i],
            send_sem=row_kv_s.at[d, g, i], recv_sem=row_kv_r.at[1 - d, g, i],
            device_id=(row_to[d], c), device_id_type=MESH)

    def row_wait(g, d, i):
        arrived(row_has[d], lambda: pltpu.make_async_remote_copy(
            src_ref=row_kv.at[d, g, i], dst_ref=row_kv.at[d, g, i],
            send_sem=row_kv_s.at[d, g, i], recv_sem=row_kv_r.at[d, g, i],
            device_id=(row_to[d], c), device_id_type=MESH))

    def tile_of(g, piece, i):
        if piece == 1:
            return (k_ref, v_ref)[i][:, lanes(g)].astype(f32).reshape(tr, tc, LANES)
        return row_kv[0 if piece == 0 else 1, g, i].astype(f32).reshape(tr, tc, LANES)

    def col_copy(g, piece, d):
        return lambda: pltpu.make_async_remote_copy(
            src_ref=col_out.at[d, g, piece], dst_ref=col_kv.at[1 - d, g, piece],
            send_sem=col_kv_s.at[d, g, piece], recv_sem=col_kv_r.at[1 - d, g, piece],
            device_id=(r, col_to[d]), device_id_type=MESH)

    def col_send(g, piece):
        for i in range(2):
            tile = tile_of(g, piece, i)
            col_out[0, g, piece, i] = tile[:, :rad].reshape(half, LANES).astype(bf16)
            col_out[1, g, piece, i] = tile[:, tc - rad:].reshape(half, LANES).astype(bf16)
        for d in range(2):
            send(col_has[d], col_copy(g, piece, d))

    def col_wait(g):
        for piece in range(3):
            for d in range(2):
                arrived(col_has[d], (lambda piece, d: lambda: pltpu.make_async_remote_copy(
                    src_ref=col_kv.at[d, g, piece], dst_ref=col_kv.at[d, g, piece],
                    send_sem=col_kv_s.at[d, g, piece], recv_sem=col_kv_r.at[d, g, piece],
                    device_id=(r, col_to[d]), device_id_type=MESH))(piece, d))

    def row_stage(g):
        for d in range(2):
            for i in range(2):
                row_wait(g, d, i)
        col_send(g, 0)
        col_send(g, 2)

    def window(g, i):
        parts = []
        for piece in range(3):
            left = col_kv[0, g, piece, i].astype(f32).reshape(tr, rad, LANES)
            right = col_kv[1, g, piece, i].astype(f32).reshape(tr, rad, LANES)
            parts.append(jnp.concatenate([left, tile_of(g, piece, i), right], axis=1))
        return jnp.concatenate(parts, axis=0).reshape(span, LANES).astype(bf16)

    def stacked(matrix, scale):
        lane = lax.broadcasted_iota(jnp.int32, (nq, LANES), 1)
        wide = matrix.astype(f32) * scale
        return jnp.concatenate(
            [jnp.where(lane // hd == h, wide, 0.0) for h in range(per)], axis=0).astype(bf16)

    def occupied_at(i, j):
        at_row, at_col = r + i - 1, c + j - 1
        inside = (at_row >= 0) & (at_row < n_row) & (at_col >= 0) & (at_col < n_col)
        value = occ_ref[jnp.clip(at_row, 0, n_row - 1), jnp.clip(at_col, 0, n_col - 1)]
        return jnp.where(inside, value, 0)

    def expand_bias():
        fill = jnp.zeros((heads, pc - win), f32)
        parts = []
        for a in range(win):
            parts += [bias_ref[a], fill]
        flat_ref[...] = jnp.concatenate(parts + [jnp.zeros((heads, span - win * pc), f32)], axis=1)
        lane = lax.broadcasted_iota(jnp.int32, (tc, span), 1)
        key_col = lax.rem(lane, pc)
        key_row = lane // pc
        query_col = lax.broadcasted_iota(jnp.int32, (tc, span), 0)
        off_col = key_col - query_col
        ok_col = (off_col >= 0) & (off_col <= 2 * rad)
        in_row = (key_row >= rad).astype(jnp.int32) + (key_row >= rad + tr).astype(jnp.int32)
        in_col = (key_col >= rad).astype(jnp.int32) + (key_col >= rad + tc).astype(jnp.int32)
        tile = 3 * in_row + in_col
        key_ok = jnp.zeros((tc, span), jnp.int32)
        for i in range(3):
            for j in range(3):
                key_ok = jnp.where(tile == 3 * i + j, occupied_at(i, j), key_ok)
        ok_col = ok_col & (key_ok > 0)

        def one_head(h, _):
            base = jnp.broadcast_to(flat_ref[pl.ds(h, 1), :], (tc, span))
            base = skew_rows(base, 1)
            for qr in range(tr):
                off_row = key_row - qr
                ok = ok_col & (off_row >= 0) & (off_row <= 2 * rad)
                moved = pltpu.roll(base, (pc * qr) % span, 1) if qr else base
                bias_full[h, qr] = jnp.where(ok, moved, MASKED)
            return 0

        lax.fori_loop(0, heads, one_head, 0)

    def compute(g):
        kw = window(g, 0)
        vw = window(g, 1)
        qs = stacked(q_ref[:, lanes(g)], hd ** -0.5)
        gs = stacked(g_ref[:, lanes(g)], 1.0)
        nt = (((1,), (1,)), ((), ()))
        s_buf[...] = lax.dot_general(qs, kw, nt, preferred_element_type=f32)
        gw_buf[...] = lax.dot_general(gs, vw, nt, preferred_element_type=f32)
        bias_acc[...] = jnp.zeros_like(bias_acc)
        own = occ_ref[r, c].astype(f32)

        for qr in range(tr):
            for h in range(per):
                at = h * nq + qr * tc
                s = s_buf[pl.ds(at, tc), :] + bias_full[g * per + h, qr]
                e = jnp.exp(s - jnp.max(s, axis=1, keepdims=True))
                w = e * (own / jnp.sum(e, axis=1, keepdims=True))
                gw = gw_buf[pl.ds(at, tc), :]
                ds = w * (gw - jnp.sum(w * gw, axis=1, keepdims=True))
                w_buf[pl.ds(at, tc), :] = w.astype(bf16)
                ds_buf[pl.ds(at, tc), :] = ds.astype(bf16)
                bias_acc[h] += pltpu.roll(ds, (span - pc * qr) % span, 1) if qr else ds

        for h in range(per):
            total = jnp.sum(skew_rows(bias_acc[h], -1), axis=0, keepdims=True)
            bias_cols[c, pl.ds(g * per + h, 1), :] = total
        ds_low = ds_buf[...]
        tn = (((0,), (0,)), ((), ()))
        dq = jnp.dot(ds_low, kw, preferred_element_type=f32) * (hd ** -0.5)
        lane = lax.broadcasted_iota(jnp.int32, (nq, LANES), 1)
        merged = dq[:nq]
        for h in range(1, per):
            merged = jnp.where(lane // hd == h, dq[h * nq:(h + 1) * nq], merged)
        dq_ref[:, lanes(g)] = merged.astype(bf16)
        for i, (left, right) in enumerate(((ds_low, qs), (w_buf[...], gs))):
            full = lax.dot_general(left, right, tn, preferred_element_type=f32)
            full = full.reshape(pr, pc, LANES)
            grad_col_out[0, g, i] = full[:, :rad].reshape(pr * rad, LANES).astype(bf16)
            grad_col_out[1, g, i] = full[:, rad + tc:].reshape(pr * rad, LANES).astype(bf16)
            mid[g, i] = full[:, rad:rad + tc]
        for d in range(2):
            send(col_has[d], (lambda d: lambda: pltpu.make_async_remote_copy(
                src_ref=grad_col_out.at[d, g], dst_ref=grad_col_in.at[1 - d, g],
                send_sem=gc_s.at[d, g], recv_sem=gc_r.at[1 - d, g],
                device_id=(r, col_to[d]), device_id_type=MESH))(d))

    def col_return(g):
        for d in range(2):
            arrived(col_has[d], (lambda d: lambda: pltpu.make_async_remote_copy(
                src_ref=grad_col_in.at[d, g], dst_ref=grad_col_in.at[d, g],
                send_sem=gc_s.at[d, g], recv_sem=gc_r.at[d, g],
                device_id=(r, col_to[d]), device_id_type=MESH))(d))
        for i in range(2):
            sides = [grad_col_in[d, g, i].astype(f32).reshape(pr, rad, LANES) for d in range(2)]
            if tc == 2 * rad:
                total = mid[g, i] + jnp.concatenate(sides, axis=1)
            else:
                gap = jnp.zeros((pr, tc - rad, LANES), f32)
                total = (mid[g, i] + jnp.concatenate([sides[0], gap], axis=1)
                         + jnp.concatenate([gap, sides[1]], axis=1))
            grad_row_out[0, g, i] = total[:rad].reshape(nq, LANES).astype(bf16)
            grad_row_out[1, g, i] = total[rad + tr:].reshape(nq, LANES).astype(bf16)
            mid[g, i] = total
        for d in range(2):
            send(row_has[d], (lambda d: lambda: pltpu.make_async_remote_copy(
                src_ref=grad_row_out.at[d, g], dst_ref=grad_row_in.at[1 - d, g],
                send_sem=gr_s.at[d, g], recv_sem=gr_r.at[1 - d, g],
                device_id=(row_to[d], c), device_id_type=MESH))(d))

    def store(src, dst):
        copy = pltpu.make_async_copy(src, dst, out_s.at[len(stores)])
        copy.start()
        stores.append(copy)

    def finish(g):
        for d in range(2):
            arrived(row_has[d], (lambda d: lambda: pltpu.make_async_remote_copy(
                src_ref=grad_row_in.at[d, g], dst_ref=grad_row_in.at[d, g],
                send_sem=gr_s.at[d, g], recv_sem=gr_r.at[d, g],
                device_id=(row_to[d], c), device_id_type=MESH))(d))
        for i, out in enumerate((dk_ref, dv_ref)):
            total = mid[g, i, pl.ds(rad, tr)].reshape(nq, LANES)
            total = total + grad_row_in[0, g, i].astype(f32) + grad_row_in[1, g, i].astype(f32)
            out[:, lanes(g)] = total.astype(bf16)
            store(out.at[:, lanes(g)], (dk_hbm, dv_hbm)[i].at[:, lanes(g)])

    for g in range(groups):
        for d in range(2):
            for i in range(2):
                send(row_has[d], row_copy(g, d, i))
    for g in range(groups):
        col_send(g, 1)
    clear_missing()
    for load in loads[2:]:
        load.wait()
    expand_bias()
    row_stage(0)
    for g in range(groups):
        if g + 1 < groups:
            row_stage(g + 1)
        col_wait(g)
        compute(g)
        if g >= 1:
            col_return(g - 1)
        if g >= 2:
            finish(g - 2)

    store(dq_ref, dq_hbm)

    def bias_copies(buf, mine, count, send_sem, recv_sem, device):
        return [pltpu.make_async_remote_copy(
            src_ref=buf.at[mine], dst_ref=buf.at[mine],
            send_sem=send_sem.at[step], recv_sem=recv_sem.at[step],
            device_id=device(lax.rem(mine + step, count)), device_id_type=MESH)
            for step in range(1, count)]

    def bias_waits(buf, mine, count, send_sem, recv_sem, device):
        for step in range(1, count):
            source = lax.rem(mine + count - step, count)
            pltpu.make_async_remote_copy(
                src_ref=buf.at[source], dst_ref=buf.at[source],
                send_sem=send_sem.at[step], recv_sem=recv_sem.at[step],
                device_id=device(source), device_id_type=MESH).wait_recv()

    by_col = (bias_cols, c, n_col, bc_s, bc_r, lambda at: (r, at))
    by_row = (bias_rows, r, n_row, br_s, br_r, lambda at: (at, c))
    col_copies = bias_copies(*by_col)
    for copy in col_copies:
        copy.start()
    col_return(groups - 1)
    if groups >= 2:
        finish(groups - 2)
    bias_waits(*by_col)
    total = bias_cols[0]
    for at in range(1, n_col):
        total = total + bias_cols[at]
    bias_rows[r] = total
    row_copies = bias_copies(*by_row)
    for copy in row_copies:
        copy.start()
    finish(groups - 1)
    bias_waits(*by_row)
    total = bias_rows[0]
    for at in range(1, n_row):
        total = total + bias_rows[at]
    for a in range(win):
        db_ref[a] = total[:, a * pc:a * pc + win]
    store(db_ref, db_hbm)
    for copy in col_copies + row_copies:
        copy.wait_send()
    for copy in stores:
        copy.wait()
    for cond, make in pending:
        @pl.when(cond)
        def _():
            make().wait_send()


def writer(*refs):
    count = (len(refs) - 2) // 3
    ins, outs, held = refs[:count], refs[count:2 * count], refs[2 * count:3 * count]
    in_sems, out_sems = refs[3 * count:]
    reads = [pltpu.make_async_copy(a, b, in_sems.at[i]) for i, (a, b) in enumerate(zip(ins, held))]
    writes = [pltpu.make_async_copy(a, b, out_sems.at[i]) for i, (a, b) in enumerate(zip(held, outs))]
    for read in reads:
        read.start()
    for read, write in zip(reads, writes):
        read.wait()
        write.start()
    for write in writes:
        write.wait()


def shards(n_row, n_col, queries, keys, values, grad_out, rel_bias, occupied):
    tr, tc, width = queries.shape
    heads, win, _ = rel_bias.shape
    rad = (win - 1) // 2
    pr, pc = tr + 2 * rad, tc + 2 * rad
    span = pr * pc
    nq = tr * tc
    groups = width // LANES
    per = heads // groups
    half = rad * tr
    f32, bf16 = jnp.float32, jnp.bfloat16
    hbm = pl.BlockSpec(memory_space=pltpu.HBM)
    dma = pltpu.SemaphoreType.DMA
    token = jax.ShapeDtypeStruct((nq, width), bf16)
    results = (token, token, token, jax.ShapeDtypeStruct((win, heads, win), f32))
    held = [pltpu.VMEM(result.shape, result.dtype) for result in results]
    cfg = (n_row, n_col, tr, tc, rad, heads, width)
    dq, dk, dv, db = pl.pallas_call(
        functools.partial(kernel, cfg),
        out_shape=results,
        in_specs=[hbm] * 6,
        out_specs=(hbm,) * 4,
        scratch_shapes=[pltpu.VMEM((nq, width), bf16)] * 4 + [
            pltpu.VMEM((win, heads, win), f32),
            pltpu.SMEM(occupied.shape, jnp.int32),
        ] + held + [
            dma((6,)), dma((2 * groups + 2,)),
            pltpu.VMEM((2, groups, 2, nq, LANES), bf16),
            pltpu.VMEM((2, groups, 3, 2, half, LANES), bf16),
            pltpu.VMEM((2, groups, 3, 2, half, LANES), bf16),
            pltpu.VMEM((2, groups, 2, pr * rad, LANES), bf16),
            pltpu.VMEM((2, groups, 2, pr * rad, LANES), bf16),
            pltpu.VMEM((2, groups, 2, nq, LANES), bf16),
            pltpu.VMEM((2, groups, 2, nq, LANES), bf16),
            pltpu.VMEM((groups, 2, pr, tc, LANES), f32),
            pltpu.VMEM((heads, span), f32),
            pltpu.VMEM((heads, tr, tc, span), f32),
            pltpu.VMEM((per * nq, span), f32),
            pltpu.VMEM((per * nq, span), f32),
            pltpu.VMEM((per * nq, span), bf16),
            pltpu.VMEM((per * nq, span), bf16),
            pltpu.VMEM((per, tc, span), f32),
            pltpu.VMEM((n_col, heads, span), f32),
            pltpu.VMEM((n_row, heads, span), f32),
            dma((2, groups, 2)), dma((2, groups, 2)),
            dma((2, groups, 3)), dma((2, groups, 3)),
            dma((2, groups)), dma((2, groups)),
            dma((2, groups)), dma((2, groups)),
            dma((n_col,)), dma((n_col,)),
            dma((n_row,)), dma((n_row,)),
        ],
        compiler_params=pltpu.CompilerParams(
            collective_id=0, has_side_effects=True),
    )(
        queries.reshape(nq, width), keys.reshape(nq, width), values.reshape(nq, width),
        grad_out.reshape(nq, width), jnp.transpose(rel_bias, (1, 0, 2)), occupied,
    )
    dq, dk, dv, db = pl.pallas_call(
        writer,
        out_shape=results,
        in_specs=[hbm] * 4,
        out_specs=(hbm,) * 4,
        scratch_shapes=held + [dma((4,)), dma((4,))],
    )(dq, dk, dv, db)
    shape = (tr, tc, width)
    return dq.reshape(shape), dk.reshape(shape), dv.reshape(shape), jnp.transpose(db, (1, 0, 2))


def solution(mesh):
    tokens = P("row", "col", None)
    return jax.shard_map(
        functools.partial(shards, mesh.shape["row"], mesh.shape["col"]),
        mesh=mesh,
        in_specs=(tokens,) * 4 + (P(), P()),
        out_specs=(tokens,) * 3 + (P(),),
        check_vma=False,
    )
```

```python
import functools

import jax
import jax.numpy as jnp
from jax import lax
from jax.experimental import pallas as pl
from jax.experimental.pallas import tpu as pltpu
from jax.sharding import PartitionSpec as P

MESH = pl.DeviceIdType.MESH
LANES = 128
MASKED = -1e30


def skew_rows(block, direction):
    row = lax.broadcasted_iota(jnp.int32, block.shape, 0)
    span = block.shape[1]
    bit = 1
    while bit < block.shape[0]:
        moved = pltpu.roll(block, (direction * bit) % span, 1)
        block = jnp.where((row & bit) != 0, moved, block)
        bit *= 2
    return block


def kernel(
    cfg,
    q_hbm, k_hbm, v_hbm, g_hbm, bias_hbm, occ_hbm,
    dq_hbm, dk_hbm, dv_hbm, db_hbm,
    q_ref, k_ref, v_ref, g_ref, bias_ref, occ_ref, dq_ref, dk_ref, dv_ref, db_ref, in_s, out_s,
    row_kv, col_kv, col_out, grad_col_out, grad_col_in, grad_row_out, grad_row_in,
    mid, flat_ref, bias_full, s_buf, gw_buf, w_buf, ds_buf, bias_acc, bias_cols, bias_rows,
    row_kv_s, row_kv_r, col_kv_s, col_kv_r, gc_s, gc_r, gr_s, gr_r, bc_s, bc_r, br_s, br_r,
):
    n_row, n_col, tr, tc, rad, heads, width = cfg
    win = 2 * rad + 1
    hd = width // heads
    per = LANES // hd
    groups = width // LANES
    pr, pc = tr + 2 * rad, tc + 2 * rad
    span = pr * pc
    nq = tr * tc
    half = rad * tr
    f32, bf16 = jnp.float32, jnp.bfloat16
    r = lax.axis_index("row")
    c = lax.axis_index("col")
    row_has = (r > 0, r < n_row - 1)
    row_to = (r - 1, r + 1)
    col_has = (c > 0, c < n_col - 1)
    col_to = (c - 1, c + 1)

    moves = ((k_hbm, k_ref), (v_hbm, v_ref), (occ_hbm, occ_ref), (bias_hbm, bias_ref), (q_hbm, q_ref), (g_hbm, g_ref))
    loads = [pltpu.make_async_copy(a, b, in_s.at[i]) for i, (a, b) in enumerate(moves)]
    for load in loads:
        load.start()

    barrier = pltpu.get_barrier_semaphore()
    for step in range(1, n_col):
        pl.semaphore_signal(barrier, 1, device_id=(r, lax.rem(c + step, n_col)), device_id_type=MESH)
    for step in range(1, n_row):
        pl.semaphore_signal(barrier, 1, device_id=(lax.rem(r + step, n_row), c), device_id_type=MESH)
    pl.semaphore_wait(barrier, n_col + n_row - 2)

    for load in loads[:2]:
        load.wait()
    pending = []
    stores = []

    def send(cond, make):
        @pl.when(cond)
        def _():
            make().start()

        pending.append((cond, make))

    def arrived(cond, make):
        @pl.when(cond)
        def _():
            make().wait_recv()

    def lanes(g):
        return pl.ds(g * LANES, LANES)

    def clear_missing():
        for d in range(2):
            @pl.when(jnp.logical_not(row_has[d]))
            def _():
                row_kv[d] = jnp.zeros_like(row_kv[d])
                grad_row_in[d] = jnp.zeros_like(grad_row_in[d])

            @pl.when(jnp.logical_not(col_has[d]))
            def _():
                col_kv[d] = jnp.zeros_like(col_kv[d])
                grad_col_in[d] = jnp.zeros_like(grad_col_in[d])

    def row_copy(g, d, i):
        src = (k_ref, v_ref)[i]
        return lambda: pltpu.make_async_remote_copy(
            src_ref=src.at[:, lanes(g)], dst_ref=row_kv.at[1 - d, g, i],
            send_sem=row_kv_s.at[d, g, i], recv_sem=row_kv_r.at[1 - d, g, i],
            device_id=(row_to[d], c), device_id_type=MESH)

    def row_wait(g, d, i):
        arrived(row_has[d], lambda: pltpu.make_async_remote_copy(
            src_ref=row_kv.at[d, g, i], dst_ref=row_kv.at[d, g, i],
            send_sem=row_kv_s.at[d, g, i], recv_sem=row_kv_r.at[d, g, i],
            device_id=(row_to[d], c), device_id_type=MESH))

    def tile_of(g, piece, i):
        if piece == 1:
            return (k_ref, v_ref)[i][:, lanes(g)].astype(f32).reshape(tr, tc, LANES)
        return row_kv[0 if piece == 0 else 1, g, i].astype(f32).reshape(tr, tc, LANES)

    def col_copy(g, piece, d):
        return lambda: pltpu.make_async_remote_copy(
            src_ref=col_out.at[d, g, piece], dst_ref=col_kv.at[1 - d, g, piece],
            send_sem=col_kv_s.at[d, g, piece], recv_sem=col_kv_r.at[1 - d, g, piece],
            device_id=(r, col_to[d]), device_id_type=MESH)

    def col_send(g, piece):
        for i in range(2):
            tile = tile_of(g, piece, i)
            col_out[0, g, piece, i] = tile[:, :rad].reshape(half, LANES).astype(bf16)
            col_out[1, g, piece, i] = tile[:, tc - rad:].reshape(half, LANES).astype(bf16)
        for d in range(2):
            send(col_has[d], col_copy(g, piece, d))

    def col_wait(g):
        for piece in range(3):
            for d in range(2):
                arrived(col_has[d], (lambda piece, d: lambda: pltpu.make_async_remote_copy(
                    src_ref=col_kv.at[d, g, piece], dst_ref=col_kv.at[d, g, piece],
                    send_sem=col_kv_s.at[d, g, piece], recv_sem=col_kv_r.at[d, g, piece],
                    device_id=(r, col_to[d]), device_id_type=MESH))(piece, d))

    def row_stage(g):
        for d in range(2):
            for i in range(2):
                row_wait(g, d, i)
        col_send(g, 0)
        col_send(g, 2)

    def window(g, i):
        parts = []
        for piece in range(3):
            left = col_kv[0, g, piece, i].astype(f32).reshape(tr, rad, LANES)
            right = col_kv[1, g, piece, i].astype(f32).reshape(tr, rad, LANES)
            parts.append(jnp.concatenate([left, tile_of(g, piece, i), right], axis=1))
        return jnp.concatenate(parts, axis=0).reshape(span, LANES).astype(bf16)

    def stacked(matrix, scale):
        lane = lax.broadcasted_iota(jnp.int32, (nq, LANES), 1)
        wide = matrix.astype(f32) * scale
        return jnp.concatenate(
            [jnp.where(lane // hd == h, wide, 0.0) for h in range(per)], axis=0).astype(bf16)

    def occupied_at(i, j):
        at_row, at_col = r + i - 1, c + j - 1
        inside = (at_row >= 0) & (at_row < n_row) & (at_col >= 0) & (at_col < n_col)
        value = occ_ref[jnp.clip(at_row, 0, n_row - 1), jnp.clip(at_col, 0, n_col - 1)]
        return jnp.where(inside, value, 0)

    def expand_bias():
        fill = jnp.zeros((heads, pc - win), f32)
        parts = []
        for a in range(win):
            parts += [bias_ref[a], fill]
        flat_ref[...] = jnp.concatenate(parts + [jnp.zeros((heads, span - win * pc), f32)], axis=1)
        lane = lax.broadcasted_iota(jnp.int32, (tc, span), 1)
        key_col = lax.rem(lane, pc)
        key_row = lane // pc
        query_col = lax.broadcasted_iota(jnp.int32, (tc, span), 0)
        off_col = key_col - query_col
        ok_col = (off_col >= 0) & (off_col <= 2 * rad)
        in_row = (key_row >= rad).astype(jnp.int32) + (key_row >= rad + tr).astype(jnp.int32)
        in_col = (key_col >= rad).astype(jnp.int32) + (key_col >= rad + tc).astype(jnp.int32)
        tile = 3 * in_row + in_col
        key_ok = jnp.zeros((tc, span), jnp.int32)
        for i in range(3):
            for j in range(3):
                key_ok = jnp.where(tile == 3 * i + j, occupied_at(i, j), key_ok)
        ok_col = ok_col & (key_ok > 0)

        def one_head(h, _):
            base = jnp.broadcast_to(flat_ref[pl.ds(h, 1), :], (tc, span))
            base = skew_rows(base, 1)
            for qr in range(tr):
                off_row = key_row - qr
                ok = ok_col & (off_row >= 0) & (off_row <= 2 * rad)
                moved = pltpu.roll(base, (pc * qr) % span, 1) if qr else base
                bias_full[h, qr] = jnp.where(ok, moved, MASKED)
            return 0

        lax.fori_loop(0, heads, one_head, 0)

    def compute(g):
        kw = window(g, 0)
        vw = window(g, 1)
        qs = stacked(q_ref[:, lanes(g)], hd ** -0.5)
        gs = stacked(g_ref[:, lanes(g)], 1.0)
        nt = (((1,), (1,)), ((), ()))
        s_buf[...] = lax.dot_general(qs, kw, nt, preferred_element_type=f32)
        gw_buf[...] = lax.dot_general(gs, vw, nt, preferred_element_type=f32)
        bias_acc[...] = jnp.zeros_like(bias_acc)
        own = occ_ref[r, c].astype(f32)

        for qr in range(tr):
            for h in range(per):
                at = h * nq + qr * tc
                s = s_buf[pl.ds(at, tc), :] + bias_full[g * per + h, qr]
                e = jnp.exp(s - jnp.max(s, axis=1, keepdims=True))
                w = e * (own / jnp.sum(e, axis=1, keepdims=True))
                gw = gw_buf[pl.ds(at, tc), :]
                ds = w * (gw - jnp.sum(w * gw, axis=1, keepdims=True))
                w_buf[pl.ds(at, tc), :] = w.astype(bf16)
                ds_buf[pl.ds(at, tc), :] = ds.astype(bf16)
                bias_acc[h] += pltpu.roll(ds, (span - pc * qr) % span, 1) if qr else ds

        for h in range(per):
            total = jnp.sum(skew_rows(bias_acc[h], -1), axis=0, keepdims=True)
            bias_cols[c, g, pl.ds(h, 1), :] = total
        ds_low = ds_buf[...]
        tn = (((0,), (0,)), ((), ()))
        dq = jnp.dot(ds_low, kw, preferred_element_type=f32) * (hd ** -0.5)
        lane = lax.broadcasted_iota(jnp.int32, (nq, LANES), 1)
        merged = dq[:nq]
        for h in range(1, per):
            merged = jnp.where(lane // hd == h, dq[h * nq:(h + 1) * nq], merged)
        dq_ref[:, lanes(g)] = merged.astype(bf16)
        for i, (left, right) in enumerate(((ds_low, qs), (w_buf[...], gs))):
            full = lax.dot_general(left, right, tn, preferred_element_type=f32)
            full = full.reshape(pr, pc, LANES)
            grad_col_out[0, g, i] = full[:, :rad].reshape(pr * rad, LANES).astype(bf16)
            grad_col_out[1, g, i] = full[:, rad + tc:].reshape(pr * rad, LANES).astype(bf16)
            mid[g, i] = full[:, rad:rad + tc]
        for d in range(2):
            send(col_has[d], (lambda d: lambda: pltpu.make_async_remote_copy(
                src_ref=grad_col_out.at[d, g], dst_ref=grad_col_in.at[1 - d, g],
                send_sem=gc_s.at[d, g], recv_sem=gc_r.at[1 - d, g],
                device_id=(r, col_to[d]), device_id_type=MESH))(d))

    def col_return(g):
        for d in range(2):
            arrived(col_has[d], (lambda d: lambda: pltpu.make_async_remote_copy(
                src_ref=grad_col_in.at[d, g], dst_ref=grad_col_in.at[d, g],
                send_sem=gc_s.at[d, g], recv_sem=gc_r.at[d, g],
                device_id=(r, col_to[d]), device_id_type=MESH))(d))
        for i in range(2):
            sides = [grad_col_in[d, g, i].astype(f32).reshape(pr, rad, LANES) for d in range(2)]
            if tc == 2 * rad:
                total = mid[g, i] + jnp.concatenate(sides, axis=1)
            else:
                gap = jnp.zeros((pr, tc - rad, LANES), f32)
                total = (mid[g, i] + jnp.concatenate([sides[0], gap], axis=1)
                         + jnp.concatenate([gap, sides[1]], axis=1))
            grad_row_out[0, g, i] = total[:rad].reshape(nq, LANES).astype(bf16)
            grad_row_out[1, g, i] = total[rad + tr:].reshape(nq, LANES).astype(bf16)
            mid[g, i] = total
        for d in range(2):
            send(row_has[d], (lambda d: lambda: pltpu.make_async_remote_copy(
                src_ref=grad_row_out.at[d, g], dst_ref=grad_row_in.at[1 - d, g],
                send_sem=gr_s.at[d, g], recv_sem=gr_r.at[1 - d, g],
                device_id=(row_to[d], c), device_id_type=MESH))(d))

    def store(src, dst):
        copy = pltpu.make_async_copy(src, dst, out_s.at[len(stores)])
        copy.start()
        stores.append(copy)

    def finish(g):
        for d in range(2):
            arrived(row_has[d], (lambda d: lambda: pltpu.make_async_remote_copy(
                src_ref=grad_row_in.at[d, g], dst_ref=grad_row_in.at[d, g],
                send_sem=gr_s.at[d, g], recv_sem=gr_r.at[d, g],
                device_id=(row_to[d], c), device_id_type=MESH))(d))
        for i, out in enumerate((dk_ref, dv_ref)):
            total = mid[g, i, pl.ds(rad, tr)].reshape(nq, LANES)
            total = total + grad_row_in[0, g, i].astype(f32) + grad_row_in[1, g, i].astype(f32)
            out[:, lanes(g)] = total.astype(bf16)
            store(out.at[:, lanes(g)], (dk_hbm, dv_hbm)[i].at[:, lanes(g)])

    parts = (pl.ds(0, groups - 1), pl.ds(groups - 1, 1))
    bias_out = []

    def bias_copy(phase, buf, slot, step, send_sem, recv_sem, device):
        return pltpu.make_async_remote_copy(
            src_ref=buf.at[slot, parts[phase]], dst_ref=buf.at[slot, parts[phase]],
            send_sem=send_sem.at[phase, step], recv_sem=recv_sem.at[phase, step],
            device_id=device, device_id_type=MESH)

    def bias_send(phase, buf, mine, count, send_sem, recv_sem, device):
        for step in range(1, count):
            copy = bias_copy(phase, buf, mine, step, send_sem, recv_sem, device(lax.rem(mine + step, count)))
            copy.start()
            bias_out.append(copy)

    def bias_wait(phase, buf, mine, count, send_sem, recv_sem, device):
        for step in range(1, count):
            source = lax.rem(mine + count - step, count)
            bias_copy(phase, buf, source, step, send_sem, recv_sem, device(source)).wait_recv()

    def bias_sum(phase):
        total = bias_cols[0, parts[phase]]
        for at in range(1, n_col):
            total = total + bias_cols[at, parts[phase]]
        bias_rows[r, parts[phase]] = total

    by_col = (bias_cols, c, n_col, bc_s, bc_r, lambda at: (r, at))
    by_row = (bias_rows, r, n_row, br_s, br_r, lambda at: (at, c))

    for g in range(groups):
        for d in range(2):
            for i in range(2):
                send(row_has[d], row_copy(g, d, i))
    for g in range(groups):
        col_send(g, 1)
    clear_missing()
    for load in loads[2:]:
        load.wait()
    expand_bias()
    row_stage(0)
    for g in range(groups):
        if g + 1 < groups:
            row_stage(g + 1)
        col_wait(g)
        compute(g)
        if g >= groups - 2:
            bias_send(g - groups + 2, *by_col)
        if g >= 1:
            col_return(g - 1)
        if g >= 2:
            finish(g - 2)

    store(dq_ref, dq_hbm)
    bias_wait(0, *by_col)
    bias_sum(0)
    bias_send(0, *by_row)
    col_return(groups - 1)
    finish(groups - 2)
    bias_wait(1, *by_col)
    bias_sum(1)
    bias_send(1, *by_row)
    bias_wait(0, *by_row)
    finish(groups - 1)
    bias_wait(1, *by_row)
    for g in range(groups):
        total = bias_rows[0, g]
        for at in range(1, n_row):
            total = total + bias_rows[at, g]
        for a in range(win):
            db_ref[a, pl.ds(g * per, per), :] = total[:, a * pc:a * pc + win]
    store(db_ref, db_hbm)
    for copy in bias_out:
        copy.wait_send()
    for copy in stores:
        copy.wait()
    for cond, make in pending:
        @pl.when(cond)
        def _():
            make().wait_send()


def writer(*refs):
    count = (len(refs) - 2) // 3
    ins, outs, held = refs[:count], refs[count:2 * count], refs[2 * count:3 * count]
    in_sems, out_sems = refs[3 * count:]
    reads = [pltpu.make_async_copy(a, b, in_sems.at[i]) for i, (a, b) in enumerate(zip(ins, held))]
    writes = [pltpu.make_async_copy(a, b, out_sems.at[i]) for i, (a, b) in enumerate(zip(held, outs))]
    for read in reads:
        read.start()
    for read, write in zip(reads, writes):
        read.wait()
        write.start()
    for write in writes:
        write.wait()


def shards(n_row, n_col, queries, keys, values, grad_out, rel_bias, occupied):
    tr, tc, width = queries.shape
    heads, win, _ = rel_bias.shape
    rad = (win - 1) // 2
    pr, pc = tr + 2 * rad, tc + 2 * rad
    span = pr * pc
    nq = tr * tc
    groups = width // LANES
    per = heads // groups
    half = rad * tr
    f32, bf16 = jnp.float32, jnp.bfloat16
    hbm = pl.BlockSpec(memory_space=pltpu.HBM)
    dma = pltpu.SemaphoreType.DMA
    token = jax.ShapeDtypeStruct((nq, width), bf16)
    results = (token, token, token, jax.ShapeDtypeStruct((win, heads, win), f32))
    held = [pltpu.VMEM(result.shape, result.dtype) for result in results]
    cfg = (n_row, n_col, tr, tc, rad, heads, width)
    dq, dk, dv, db = pl.pallas_call(
        functools.partial(kernel, cfg),
        out_shape=results,
        in_specs=[hbm] * 6,
        out_specs=(hbm,) * 4,
        scratch_shapes=[pltpu.VMEM((nq, width), bf16)] * 4 + [
            pltpu.VMEM((win, heads, win), f32),
            pltpu.SMEM(occupied.shape, jnp.int32),
        ] + held + [
            dma((6,)), dma((2 * groups + 2,)),
            pltpu.VMEM((2, groups, 2, nq, LANES), bf16),
            pltpu.VMEM((2, groups, 3, 2, half, LANES), bf16),
            pltpu.VMEM((2, groups, 3, 2, half, LANES), bf16),
            pltpu.VMEM((2, groups, 2, pr * rad, LANES), bf16),
            pltpu.VMEM((2, groups, 2, pr * rad, LANES), bf16),
            pltpu.VMEM((2, groups, 2, nq, LANES), bf16),
            pltpu.VMEM((2, groups, 2, nq, LANES), bf16),
            pltpu.VMEM((groups, 2, pr, tc, LANES), f32),
            pltpu.VMEM((heads, span), f32),
            pltpu.VMEM((heads, tr, tc, span), f32),
            pltpu.VMEM((per * nq, span), f32),
            pltpu.VMEM((per * nq, span), f32),
            pltpu.VMEM((per * nq, span), bf16),
            pltpu.VMEM((per * nq, span), bf16),
            pltpu.VMEM((per, tc, span), f32),
            pltpu.VMEM((n_col, groups, per, span), f32),
            pltpu.VMEM((n_row, groups, per, span), f32),
            dma((2, groups, 2)), dma((2, groups, 2)),
            dma((2, groups, 3)), dma((2, groups, 3)),
            dma((2, groups)), dma((2, groups)),
            dma((2, groups)), dma((2, groups)),
            dma((2, n_col)), dma((2, n_col)),
            dma((2, n_row)), dma((2, n_row)),
        ],
        compiler_params=pltpu.CompilerParams(
            collective_id=0, has_side_effects=True),
    )(
        queries.reshape(nq, width), keys.reshape(nq, width), values.reshape(nq, width),
        grad_out.reshape(nq, width), jnp.transpose(rel_bias, (1, 0, 2)), occupied,
    )
    dq, dk, dv, db = pl.pallas_call(
        writer,
        out_shape=results,
        in_specs=[hbm] * 4,
        out_specs=(hbm,) * 4,
        scratch_shapes=held + [dma((4,)), dma((4,))],
    )(dq, dk, dv, db)
    shape = (tr, tc, width)
    return dq.reshape(shape), dk.reshape(shape), dv.reshape(shape), jnp.transpose(db, (1, 0, 2))


def solution(mesh):
    tokens = P("row", "col", None)
    return jax.shard_map(
        functools.partial(shards, mesh.shape["row"], mesh.shape["col"]),
        mesh=mesh,
        in_specs=(tokens,) * 4 + (P(), P()),
        out_specs=(tokens,) * 3 + (P(),),
        check_vma=False,
    )
```
